32 devices in a mesh: ctx: 8 (over z, x), head: 4 (over y, core).
Axes of the slice: x: 2, y: 2, z: 4, core: 2. Of those that a mesh axis runs over, the one named last changes fastest.
Arguments:
- tokens: bfloat16 [16, 8192], P(None, 'ctx'), may hold values from -1000 to 1000
- norm_gain: float32 [8192], P('ctx'), may hold values from 0.5 to 2
- w_query: bfloat16 [8192, 4096], P('ctx', 'head'), may hold values from -0.0625 to 0.0625
- w_out: bfloat16 [4096, 8192], P('head', 'ctx'), may hold values from -0.09375 to 0.09375
- kv_cache: bfloat16 [16, 4, 128, 64, 256], P(None, 'head', 'ctx'), may hold values from -128 to 128
- page_ids: int32 [2, 16, 4, 32], P(None, None, 'head'), may hold values from 0 to 127, as said below
Outputs:
- block_outputs: bfloat16 [2, 16, 8192], P(None, None, 'ctx')
The draws below stay inside these ranges and needn't reach their ends.
Inputs may be any that keep to these rules, and one draw needn't show every extreme that they name: `page_ids`: entries 0 to 15 and 16 to 31 of each list are its two halves. The 32 pages of one list are distinct. Block b holds pages b * 16 to (b + 1) * 16 - 1; within one half at most 2 pages lie in one block, and every half has exactly 2 pages in some block.
All inputs are finite; a program needn't handle non-finite values.
Results may differ from the reference program's by a relative error of at most 0.019.
Values may be sent and summed in bfloat16 or wider, within the bound.
A program may use at most 64 MiB of HBM per device.

```python
import math
import jax
import jax.numpy as jnp
from jax import lax

D = 8192
HD = 128
GROUP = 8
ROWS = 16
PAGE = 64
PAGES_DEV = 16
SEL = 32
STEPS = 2
KVH = 4
HQ = 32
PAGES = 128


hot_count = 3


def draw_tokens(key, part):
    key_base, key_row, key_col = jax.random.split(key, 3)
    column = jnp.arange(D, dtype=jnp.float32) / D
    jitter = jnp.exp(jax.random.uniform(key_col, (1, D), jnp.float32, -0.35, 0.35))
    col_scale = jnp.exp(column * math.log(10.0))[None, :] * jitter
    cells = jnp.clip(jax.random.normal(key_base, (ROWS, D), jnp.float32), -4.0, 4.0)
    row_scale = jnp.exp(jax.random.uniform(key_row, (ROWS, 1), jnp.float32, 0.0, math.log(10.0)))
    return (cells * row_scale * col_scale).astype(jnp.bfloat16)


def draw_kv_cache(key, part):
    key_base = jax.random.fold_in(key, 0)
    shape = (ROWS, KVH, PAGES, PAGE, 2 * HD)
    cells = jnp.clip(jax.random.normal(key_base, shape, jnp.float32), -6.0, 6.0)
    return cells.astype(jnp.bfloat16)


def shuffled_owners(one_key):
    return jax.random.permutation(one_key, PAGES // PAGES_DEV)


def draw_page_ids(key, part):
    owner_total = PAGES // PAGES_DEV
    half_len = SEL // 2
    key_hot, key_score, key_count, key_base, key_stride, key_shuffle = jax.random.split(key, 6)
    hot_order = jax.vmap(shuffled_owners)(jax.random.split(key_hot, KVH)).astype(jnp.int32)
    hot_flag = (hot_order < hot_count).astype(jnp.int32)
    lead = (STEPS, ROWS, KVH, 2)
    owner_score = jax.random.randint(key_score, lead + (owner_total,), 0, 65536) + hot_flag[None, None, :, None, :] * 65536
    owner_score = owner_score * owner_total + jnp.arange(owner_total, dtype=jnp.int32)
    owner_order = jnp.argsort(-owner_score, axis=-1, stable=True).astype(jnp.int32)
    least = max(1, half_len - owner_total)
    doubled = jax.random.randint(key_count, lead + (1,), least, half_len // 2 + 1)
    position = jnp.arange(half_len, dtype=jnp.int32)
    paired = position < 2 * doubled
    owner_slot = jnp.where(paired, position // 2, position - doubled)
    second = jnp.where(paired, position % 2, 0)
    owners = jnp.take_along_axis(owner_order, owner_slot, axis=-1)
    base_page = jax.random.randint(key_base, (STEPS, ROWS, KVH, 1, owner_total), 0, PAGES_DEV)
    stride = 2 * jax.random.randint(key_stride, (STEPS, ROWS, KVH, 1, owner_total), 0, PAGES_DEV // 2) + 1
    base_pick = jnp.take_along_axis(jnp.broadcast_to(base_page, lead + (owner_total,)), owners, axis=-1)
    stride_pick = jnp.take_along_axis(jnp.broadcast_to(stride, lead + (owner_total,)), owners, axis=-1)
    which_half = jnp.arange(2, dtype=jnp.int32)[:, None]
    offset = which_half * 2 + second
    local_page = (base_pick + offset * stride_pick) % PAGES_DEV
    chosen = owners * PAGES_DEV + local_page
    shuffle_score = jax.random.randint(key_shuffle, lead + (half_len,), 0, 65536) * half_len + position
    shuffle = jnp.argsort(shuffle_score, axis=-1, stable=True).astype(jnp.int32)
    chosen = jnp.take_along_axis(chosen, shuffle, axis=-1)
    return chosen.reshape(STEPS, ROWS, KVH, SEL).astype(jnp.int32)


def levels(key, dims, pieces, smallest, top_value):
    def one(axis_at, shards_of):
        draws = jax.random.uniform(jax.random.fold_in(jax.random.fold_in(key, 6), axis_at), (shards_of,), jnp.float32, smallest / len(pieces), top_value / len(pieces))
        return jnp.repeat(jnp.exp(draws), dims[axis_at] // shards_of).reshape((-1,) + (1,) * (len(dims) - axis_at - 1))

    level = one(*pieces[0])
    for cut in pieces[1:]:
        level = level * one(*cut)
    return level


def bell_draw(stream_key, dims, deviation, bound, shards=(), held_as=jnp.bfloat16):
    array = deviation * jax.random.normal(stream_key, dims, jnp.float32)
    if shards:
        array = array * levels(stream_key, dims, shards, -0.22, 0.18)
    return jnp.clip(array, -bound, bound).astype(held_as)


def setup_inputs(seed: int = 0) -> dict:
    key_of = jax.random.split(jax.random.key(seed), 7)
    return {
        "tokens": draw_tokens(jax.random.fold_in(key_of[6], 71), 0),
        "norm_gain": jnp.clip(jnp.exp(math.log(2.0) - 1.3862944 * jax.random.uniform(key_of[1], (D,), jnp.float32) ** levels(key_of[1], (D,), ((0, 8),), -0.2, 0.2)), 0.5, 2.0),
        "w_query": bell_draw(key_of[2], (D, HQ * HD), D ** -0.5, 0.0625, ((0, 8), (1, 4))),
        "w_out": bell_draw(key_of[3], (HQ * HD, D), (HQ * HD) ** -0.5, 0.09375, ((0, 4), (1, 8))),
        "kv_cache": draw_kv_cache(jax.random.fold_in(key_of[6], 71), 0),
        "page_ids": draw_page_ids(jax.random.fold_in(key_of[6], 71), 0),
    }


epsilon = 1e-05

def reference(tokens, norm_gain, w_query, w_out, kv_cache, page_ids):
    score_scale = 1.0 / math.sqrt(HD)
    residual = tokens
    produced = []
    for decode_step in range(STEPS):
        wide = residual.astype(jnp.float32)
        scaled = (wide * norm_gain).astype(jnp.bfloat16)
        inv_rms = 1.0 / jnp.sqrt(lax.optimization_barrier(jnp.sum(wide * wide, axis=1)) / D + epsilon)
        product = jnp.dot(scaled, w_query, preferred_element_type=jnp.float32)
        queries = (product * inv_rms[:, None]).astype(jnp.bfloat16).reshape(ROWS, KVH, GROUP, HD)
        chosen = page_ids[decode_step].astype(jnp.int32)
        fetched = jnp.take_along_axis(kv_cache, chosen[:, :, :, None, None], axis=2)
        fetched = fetched.reshape(ROWS, KVH, SEL * PAGE, 2 * HD)
        key_part = fetched[..., :HD].astype(jnp.float32)
        value_part = fetched[..., HD:].astype(jnp.float32)
        scores = jnp.einsum('rhgd,rhtd->rhgt', queries.astype(jnp.float32), key_part) * score_scale
        peak = lax.optimization_barrier(jnp.max(scores, axis=3, keepdims=True))
        weights = jnp.exp(scores - peak)
        weight_sum = lax.optimization_barrier(jnp.sum(weights, axis=3))
        rounded = lax.optimization_barrier(weights.astype(jnp.bfloat16))
        mixed = jnp.einsum('rhgt,rhtd->rhgd', rounded.astype(jnp.float32), value_part)
        attn = (mixed / weight_sum[..., None]).astype(jnp.bfloat16).reshape(ROWS, HQ * HD)
        block = jnp.dot(attn, w_out, preferred_element_type=jnp.float32).astype(jnp.bfloat16)
        produced.append(block)
        residual = (residual.astype(jnp.float32) + block.astype(jnp.float32)).astype(jnp.bfloat16)
    return jnp.stack(produced)
```

```python
import functools
import math

import jax
import jax.numpy as jnp
from jax import lax
from jax.experimental import pallas as pl
from jax.experimental.pallas import tpu as pltpu
from jax.sharding import PartitionSpec as P

def ORDER(n):
    return sorted(range(1, n), key=lambda k: (abs(2 * k - n), k))


MESH = pl.DeviceIdType.MESH
HALVES = 2
MOST = 2
SLOTS = HALVES * MOST
PARTS = 2
EPSILON = 1e-05
LOWEST = -1e30


def fold(value):
    span = value.shape[1] // PARTS
    return jnp.concatenate([value[:, p * span : (p + 1) * span] for p in range(PARTS)], axis=0)


def unfold(value):
    band = value.shape[0] // PARTS
    return jnp.concatenate([value[p * band : (p + 1) * band] for p in range(PARTS)], axis=1)


def kernel(
    ctx_count, head_count, steps, rows, heads, hd, page, pages_dev,
    ids_hbm, tokens_hbm, gain_hbm, wq_hbm, wo_hbm, kv_hbm, out_ref,
    ids_ref, tokens_ref, gain_ref, wq, wo, kv, slot_rows, slots, q_all, o_all, c_all, square_all, stat_all, q_rows, o_rows, peak_rows, sum_rows, x_ref,
    load_sems, send_sems, recv_sems,
):
    ctx = lax.axis_index("ctx")
    head = lax.axis_index("head")
    width = tokens_ref.shape[1]
    model_width = width * ctx_count
    feats = heads * hd
    band = rows // PARTS
    f32, bf16 = jnp.float32, jnp.bfloat16

    load_q = pltpu.make_async_copy(wq_hbm, wq, load_sems.at[0])
    load_kv = pltpu.make_async_copy(kv_hbm, kv, load_sems.at[1])
    load_o = pltpu.make_async_copy(wo_hbm, wo, load_sems.at[2])
    load_slots = pltpu.make_async_copy(slot_rows, slots, load_sems.at[3])
    load_tokens = pltpu.make_async_copy(tokens_hbm, tokens_ref, load_sems.at[4])
    load_gain = pltpu.make_async_copy(gain_hbm, gain_ref, load_sems.at[5])
    load_ids = pltpu.make_async_copy(ids_hbm, ids_ref, load_sems.at[6])
    load_tokens.start()
    load_gain.start()
    load_ids.start()
    load_q.start()

    def ctx_peer(k):
        return lax.rem(ctx + k, ctx_count)

    def head_peer(k):
        return lax.rem(head + k, head_count)

    barrier = pltpu.get_barrier_semaphore()
    for k in ORDER(ctx_count):
        pl.semaphore_signal(barrier, inc=1, device_id=(ctx_peer(k), head), device_id_type=MESH)
    for k in range(1, head_count):
        pl.semaphore_signal(barrier, inc=1, device_id=(ctx, head_peer(k)), device_id_type=MESH)

    load_ids.wait()
    ids = ids_ref[...].reshape(steps * rows, ids_ref.shape[3])
    local = ids - ctx * pages_dev
    none = jnp.int32(2 * pages_dev)
    left = jnp.where((local >= 0) & (local < pages_dev), local, none)
    field = lax.broadcasted_iota(jnp.int32, (steps * rows, 128), 1)
    found = jnp.zeros((steps * rows, 128), jnp.int32)
    count = jnp.zeros((steps * rows, 1), jnp.int32)
    for s in range(SLOTS):
        least = jnp.min(left, axis=1, keepdims=True)
        found = jnp.where((field == s) & (least < none), least, found)
        count = count + (least < none).astype(jnp.int32)
        left = jnp.where(left > least, left, none)
    slot_rows[...] = jnp.where(field == SLOTS, count, found)
    load_slots.start()

    def ctx_copy(held, phase, step, part, k):
        return pltpu.make_async_remote_copy(
            src_ref=held.at[step, part, ctx],
            dst_ref=held.at[step, part, ctx],
            send_sem=send_sems.at[step, phase, part],
            recv_sem=recv_sems.at[step, phase, part],
            device_id=(ctx_peer(k), head),
            device_id_type=MESH,
        )

    def head_copy(step, part, k):
        return pltpu.make_async_remote_copy(
            src_ref=c_all.at[step, part, head],
            dst_ref=c_all.at[step, part, head],
            send_sem=send_sems.at[step, 2, part],
            recv_sem=recv_sems.at[step, 2, part],
            device_id=(ctx, head_peer(k)),
            device_id_type=MESH,
        )

    def arrived(held, phase, step, part, others):
        ref = held.at[step, part, pl.ds(0, others)]
        pltpu.make_async_copy(ref, ref, recv_sems.at[step, phase, part]).wait()

    lane = lax.broadcasted_iota(jnp.int32, (band, 128), 1)
    row = lax.broadcasted_iota(jnp.int32, (band, 128), 0)
    token = lax.broadcasted_iota(jnp.int32, (heads, SLOTS * page), 1)

    def take_step(step, part):
        span = slice(part * band, (part + 1) * band)
        if step == 0:
            x = tokens_ref[...].astype(f32)[span]
        else:
            block = head_sum(step - 1, part)
            x = (x_ref[span, :] + block).astype(bf16).astype(f32)
        x_ref[span, :] = x
        squares = jnp.sum(x * x, axis=1, keepdims=True)
        square_all[step, part, ctx] = jnp.sum(jnp.where(lane == row, squares, 0.0), axis=0, keepdims=True)
        if step == 0 and part == 0:
            load_q.wait()
            load_kv.start()
            load_o.start()
        scaled = (x * gain_ref[...]).astype(bf16)
        partial = jnp.dot(scaled, wq[...], preferred_element_type=f32)
        q_all[step, part, ctx] = fold(partial).astype(bf16)
        if step == 0 and part == 0:
            pl.semaphore_wait(barrier, ctx_count + head_count - 2)
        for k in ORDER(ctx_count):
            ctx_copy(square_all, 3, step, part, k).start()
        for k in ORDER(ctx_count):
            ctx_copy(q_all, 0, step, part, k).start()

    def head_sum(step, part):
        arrived(c_all, 2, step, part, head_count - 1)
        total = c_all[step, part, 0].astype(f32)
        for k in range(1, head_count):
            total = total + c_all[step, part, k].astype(f32)
        block = unfold(total).astype(bf16)
        out_ref[step, part * band : (part + 1) * band, :] = block
        return block.astype(f32)

    def attend(step, part):
        arrived(square_all, 3, step, part, ctx_count - 1)
        square = square_all[step, part, 0]
        for k in ORDER(ctx_count):
            square = square + square_all[step, part, k]
        square = jnp.sum(jnp.where(lane == row, square, 0.0), axis=1, keepdims=True)
        inv_rms = 1.0 / jnp.sqrt(square / model_width + EPSILON)
        arrived(q_all, 0, step, part, ctx_count - 1)
        total = q_all[step, part, 0].astype(f32)
        for k in ORDER(ctx_count):
            total = total + q_all[step, part, k].astype(f32)
        query = (unfold(total) * inv_rms).astype(bf16).astype(f32)
        for h in range(heads):
            q_rows[part, h * band : (h + 1) * band, :] = query[:, h * hd : (h + 1) * hd]
        if step == 0 and part == 0:
            load_slots.wait()
            load_kv.wait()
        values = []
        all_weights = []
        all_scores = []
        for i in range(band):
            r = part * band + i
            at = step * rows + r
            both = jnp.concatenate([kv[r, slots[at, s]] for s in range(SLOTS)], axis=0)
            values.append(both[:, hd:])
            scores = lax.dot_general(
                q_rows[part, pl.ds(i, heads, stride=band), :].astype(bf16), both[:, :hd],
                (((1,), (1,)), ((), ())), preferred_element_type=f32,
            ) * (1.0 / math.sqrt(hd))
            all_scores.append(jnp.where(token < slots[at, SLOTS] * page, scores, -jnp.inf))
        for i in range(band):
            peak = jnp.maximum(jnp.max(all_scores[i], axis=1, keepdims=True), LOWEST)
            weights = jnp.exp(all_scores[i] - peak)
            all_weights.append(weights.astype(bf16))
            peak_rows[part, pl.ds(i, heads, stride=band), :] = jnp.broadcast_to(peak, (heads, 128))
            sum_rows[part, pl.ds(i, heads, stride=band), :] = jnp.broadcast_to(
                jnp.sum(weights, axis=1, keepdims=True), (heads, 128)
            )
        for i in range(band):
            o_rows[part, pl.ds(i, heads, stride=band), :] = jnp.dot(
                all_weights[i], values[i], preferred_element_type=f32
            )
        stats = jnp.zeros((band, 128), f32)
        pieces = []
        for h in range(heads):
            span = slice(h * band, (h + 1) * band)
            pieces.append(o_rows[part, span, :])
            stats = jnp.where(lane == row * heads + h, peak_rows[part, span, :], stats)
            stats = jnp.where(lane == band * heads + row * heads + h, sum_rows[part, span, :], stats)
        stat_all[step, part, ctx] = jnp.sum(stats, axis=0, keepdims=True)
        o_all[step, part, ctx] = fold(jnp.concatenate(pieces, axis=1)).astype(bf16)
        for k in ORDER(ctx_count):
            ctx_copy(stat_all, 4, step, part, k).start()
        for k in ORDER(ctx_count):
            ctx_copy(o_all, 1, step, part, k).start()

    def project(step, part):
        arrived(stat_all, 4, step, part, ctx_count - 1)
        stats = [stat_all[step, part, k] for k in range(ctx_count)]
        top = functools.reduce(jnp.maximum, stats)
        factors = [jnp.exp(jnp.where(lane[:1] < band * heads, stat - top, 0.0)) for stat in stats]
        below = sum(f * pltpu.roll(stat, 128 - band * heads, 1) for f, stat in zip(factors, stats))
        shares = [jnp.broadcast_to(f / below, (band, 128)) for f in factors]
        arrived(o_all, 1, step, part, ctx_count - 1)
        parts = [unfold(o_all[step, part, k].astype(f32)) for k in range(ctx_count)]
        mixed = []
        for h in range(heads):
            span = slice(h * hd, (h + 1) * hd)
            mine = lane == row * heads + h
            mixed.append(
                sum(
                    jnp.sum(jnp.where(mine, shares[k], 0.0), axis=1, keepdims=True) * parts[k][:, span]
                    for k in range(ctx_count)
                )
            )
        attn = jnp.concatenate(mixed, axis=1).astype(bf16)
        if step == 0 and part == 0:
            load_o.wait()
        c_all[step, part, head] = fold(jnp.dot(attn, wo[...], preferred_element_type=f32)).astype(bf16)
        for k in range(1, head_count):
            head_copy(step, part, k).start()

    load_tokens.wait()
    load_gain.wait()
    for step in range(steps):
        for part in range(PARTS):
            take_step(step, part)
        for part in range(PARTS):
            attend(step, part)
        for part in range(PARTS):
            project(step, part)
    for part in range(PARTS):
        head_sum(steps - 1, part)

    for step in range(steps):
        for part in range(PARTS):
            for k in ORDER(ctx_count):
                ctx_copy(q_all, 0, step, part, k).wait_send()
                ctx_copy(o_all, 1, step, part, k).wait_send()
                ctx_copy(square_all, 3, step, part, k).wait_send()
                ctx_copy(stat_all, 4, step, part, k).wait_send()
            for k in range(1, head_count):
                head_copy(step, part, k).wait_send()


def shards(ctx_count, head_count, tokens, norm_gain, w_query, w_out, kv_cache, page_ids):
    rows, width = tokens.shape
    steps = page_ids.shape[0]
    _, _, pages_dev, page, both = kv_cache.shape
    hd = both // 2
    heads = w_query.shape[1] // hd
    band = rows // PARTS
    sent = heads * hd // PARTS
    vmem = pl.BlockSpec(memory_space=pltpu.VMEM)
    hbm = pl.BlockSpec(memory_space=pl.ANY)
    bf16, f32 = jnp.bfloat16, jnp.float32
    return pl.pallas_call(
        functools.partial(kernel, ctx_count, head_count, steps, rows, heads, hd, page, pages_dev),
        out_shape=jax.ShapeDtypeStruct((steps, rows, width), bf16),
        in_specs=[hbm] * 6,
        out_specs=vmem,
        scratch_shapes=[
            pltpu.VMEM(page_ids.shape, jnp.int32),
            pltpu.VMEM((rows, width), bf16),
            pltpu.VMEM((1, width), f32),
            pltpu.VMEM(w_query.shape, bf16),
            pltpu.VMEM(w_out.shape, bf16),
            pltpu.VMEM((rows, pages_dev, page, both), bf16),
            pltpu.VMEM((steps * rows, 128), jnp.int32),
            pltpu.SMEM((steps * rows, 128), jnp.int32),
            pltpu.VMEM((steps, PARTS, ctx_count, rows, sent), bf16),
            pltpu.VMEM((steps, PARTS, ctx_count, rows, sent), bf16),
            pltpu.VMEM((steps, PARTS, head_count, rows, width // PARTS), bf16),
            pltpu.VMEM((steps, PARTS, ctx_count, 1, 128), f32),
            pltpu.VMEM((steps, PARTS, ctx_count, 1, 128), f32),
            pltpu.VMEM((PARTS, heads * band, hd), f32),
            pltpu.VMEM((PARTS, heads * band, hd), f32),
            pltpu.VMEM((PARTS, heads * band, 128), f32),
            pltpu.VMEM((PARTS, heads * band, 128), f32),
            pltpu.VMEM((rows, width), f32),
            pltpu.SemaphoreType.DMA((7,)),
            pltpu.SemaphoreType.DMA((steps, 5, PARTS)),
            pltpu.SemaphoreType.DMA((steps, 5, PARTS)),
        ],
        compiler_params=pltpu.CompilerParams(
            collective_id=0, has_side_effects=True, vmem_limit_bytes=40 * 1024 * 1024
        ),
    )(
        *(
            pltpu.with_memory_space_constraint(operand, pltpu.HBM)
            for operand in (
                page_ids, tokens, norm_gain.reshape(1, width), w_query, w_out,
                kv_cache.reshape(rows, pages_dev, page, both),
            )
        )
    )


def solution(mesh):
    placed = (
        P(None, "ctx"),
        P("ctx"),
        P("ctx", "head"),
        P("head", "ctx"),
        P(None, "head", "ctx", None, None),
        P(None, None, "head", None),
    )
    return jax.shard_map(
        functools.partial(shards, mesh.shape["ctx"], mesh.shape["head"]),
        mesh=mesh, in_specs=placed, out_specs=P(None, None, "ctx"), check_vma=False,
    )
```
